32 devices in a mesh: groups: 1, ex: 16 (over z, y, core), layer: 2 (over x), pb: 1.
Axes of the slice: x: 2, y: 2, z: 4, core: 2. Of those that a mesh axis runs over, the one named last changes fastest.
Arguments:
- train_grads: float32 [2, 1536, 1024], P('layer', ('groups', 'ex')), may hold values from -64 to 64
- query_grads: float32 [2, 1, 512, 1024], P('layer', 'pb', ('groups', 'ex')), may hold values from -64 to 64
- damping: float32 [2], P('layer'), may hold values from 0.05 to 0.5
Outputs:
- influence: float32 [1536, 1, 512], P(('groups', 'ex'), 'pb', 'layer')
The draws below stay inside these ranges and needn't reach their ends.
All inputs are finite; a program needn't handle non-finite values.
Results may differ from the reference program's by a relative error of at most 0.0003.
Values sent between devices are 32-bit elements; how exact they have to be, the bound alone decides.
A program may use at most 64 MiB of HBM per device.

```python
import math
import jax
import jax.numpy as jnp
from jax import lax

P_SIZE = 1024
L = 2
NEX = 1536
QH = 1
NQE = 512


def column_scales(key):
    spread = jax.random.uniform(jax.random.fold_in(key, 101), (L, P_SIZE))
    return jnp.exp(jnp.log(0.1) + spread * jnp.log(30.0))


def gradient_law(key, row_total, salt_value):
    noise_key = jax.random.fold_in(key, salt_value)
    noise_field = jax.random.truncated_normal(noise_key, -4.0, 4.0, (L, row_total, P_SIZE))
    mixed_field = noise_field + 0.5 * jnp.roll(noise_field, 1, axis=2) - 0.35 * jnp.roll(noise_field, 5, axis=2)
    row_spread = jax.random.uniform(jax.random.fold_in(key, salt_value + 1), (L, row_total, 1))
    row_scale = jnp.exp(jnp.log(0.5) + row_spread * jnp.log(4.0))
    return mixed_field * row_scale * column_scales(key)[:, None, :]


def draw_train_grads(key, part):
    return gradient_law(key, NEX, 11).astype(jnp.float32)


def draw_query_grads(key, part):
    values = gradient_law(key, QH * NQE, 29) * (P_SIZE * L) ** (-0.5)
    return values.reshape(L, QH, NQE, P_SIZE).astype(jnp.float32)


def levels(rng, dims, shards, smallest, high):
    factor_of, own = 1.0, jax.random.fold_in(rng, 6)
    for axis_at, shards_of in shards:
        heights = jnp.exp(jax.random.uniform(jax.random.fold_in(own, axis_at), (shards_of,), jnp.float32, smallest / len(shards), high / len(shards)))
        factor_of = factor_of * jnp.repeat(heights, dims[axis_at] // shards_of).reshape([-1 if axis == axis_at else 1 for axis in range(len(dims))])
    return factor_of


def setup_inputs(seed: int = 0, part: int = 0) -> dict:
    seeds = jax.random.split(jax.random.key(seed), 4)
    part_splits = jax.random.split(jax.random.fold_in(seeds[3], part), 4)
    train_grads = draw_train_grads(jax.random.fold_in(jax.random.fold_in(seeds[3], part), 71), part)
    query_grads = draw_query_grads(jax.random.fold_in(jax.random.fold_in(seeds[3], part), 71), part)
    damping = jnp.clip(jnp.exp(math.log(0.5) - 2.3025851 * jax.random.uniform(seeds[2], (L,), jnp.float32) ** levels(seeds[2], (L,), ((0, 2),), -0.2, 0.2)), 0.05, 0.5)
    return dict(train_grads=train_grads, query_grads=query_grads, damping=damping)


def solve_rows(factor, rows_in):
    inner = lax.linalg.triangular_solve(factor, rows_in, left_side=False, lower=True, transpose_a=True)
    return lax.linalg.triangular_solve(factor, inner, left_side=False, lower=True, transpose_a=False)

def reference(train_grads, query_grads, damping):
    queries = query_grads.reshape(L, QH * NQE, P_SIZE)
    identity = jnp.eye(P_SIZE, dtype=jnp.float32)
    total = jnp.zeros((NEX, QH * NQE), jnp.float32)
    for layer_index in range(L):
        grads = train_grads[layer_index]
        gram_matrix = jnp.dot(grads.T.astype(jnp.float32), grads.astype(jnp.float32), precision=lax.Precision.HIGHEST, preferred_element_type=jnp.float32)
        fisher = gram_matrix / NEX + damping[layer_index] * identity
        factor = jnp.linalg.cholesky(fisher)
        solved = solve_rows(factor, queries[layer_index])
        total = total + jnp.dot(grads.astype(jnp.float32), solved.T.astype(jnp.float32), precision=lax.Precision.HIGHEST, preferred_element_type=jnp.float32)
    return total.reshape(NEX, QH, NQE)
```

```python
import functools
import jax
import jax.numpy as jnp
import numpy as np
from jax import lax
from jax.experimental import pallas as pl
from jax.experimental.pallas import tpu as pltpu
from jax.sharding import PartitionSpec as P

BLOCK = 128
SUB = 8
NT = (((1,), (1,)), ((), ()))
NN = (((1,), (0,)), ((), ()))
TN = (((0,), (0,)), ((), ()))
MESH = pl.DeviceIdType.MESH


def halves(x):
    hi = x.astype(jnp.bfloat16)
    return hi, (x - hi.astype(jnp.float32)).astype(jnp.bfloat16)


def dot3(a, b, dims):
    ah, al = a
    bh, bl = b
    dot = functools.partial(
        lax.dot_general, dimension_numbers=dims, preferred_element_type=jnp.float32
    )
    return dot(ah, bh) + (dot(ah, bl) + dot(al, bh))


def row_of(x, i):
    return jnp.broadcast_to(x[i : i + 1, :], x.shape)


def lane_of(x, i):
    return jnp.broadcast_to(x[:, i : i + 1], x.shape)


def invert_small(cols):
    sub = lax.broadcasted_iota(jnp.int32, cols[0].shape, 0)
    for j in range(SUB):
        inv = 1.0 / row_of(cols[j], j)
        here = sub == j
        pivot_col = cols[j]
        fresh = []
        for i in range(SUB):
            if i == j:
                fresh.append(jnp.where(here, inv, -pivot_col * inv))
            else:
                scaled = row_of(cols[i], j) * inv
                fresh.append(jnp.where(here, scaled, cols[i] - pivot_col * scaled))
        cols = fresh
    return cols


def invert_block(tiles, between):
    shape = tiles[0].shape
    sub = lax.broadcasted_iota(jnp.int32, shape, 0)
    lane = lax.broadcasted_iota(jnp.int32, shape, 1)
    count = len(tiles)
    for m in range(count):
        c0 = m * SUB
        inside = (lane >= c0) & (lane < c0 + SUB)
        panel = tiles[m]
        cols = invert_small([lane_of(panel, c0 + i) for i in range(SUB)])
        panel = jnp.where(inside, jnp.where(lane == sub + c0, 1.0, 0.0), panel)
        terms = [cols[i] * row_of(panel, i) for i in range(SUB)]
        solved = tree_sum(terms)
        rows = [row_of(solved, i) for i in range(SUB)]
        fresh = list(tiles)
        fresh[m] = solved
        order = [t % count for t in range(m + 1, m + count)]
        for t in order:
            tile = tiles[t]
            terms = [lane_of(tile, c0 + i) * rows[i] for i in range(SUB)]
            fresh[t] = jnp.where(inside, 0.0, tile) - tree_sum(terms)
        tiles = fresh
        between(m)
    return tiles


def tree_sum(terms):
    while len(terms) > 1:
        terms = [a + b for a, b in zip(terms[::2], terms[1::2])]
    return terms[0]


def pair(x):
    hi, lo = halves(x)
    return jnp.concatenate([hi, lo], axis=1)


def twice(x):
    hi, lo = halves(x)
    return jnp.concatenate([hi, hi], axis=1), jnp.concatenate([lo, lo], axis=1)


def dot4(a, b, dims):
    dot = functools.partial(
        lax.dot_general, dimension_numbers=dims, preferred_element_type=jnp.float32
    )
    return dot(a, b[0]) + dot(a, b[1])


def eliminate_kernel(inv_total, all_ref, damp_ref, x_ref, q_ref, out_ref,
                     z, diag, ch, cl, dh, dl, wx, xh, xl):
    n = all_ref.shape[1]
    nq, nx = q_ref.shape[0], x_ref.shape[0]
    cols = out_ref.shape[2]
    rows = z.shape[0]
    blocks = n // BLOCK
    chunks = BLOCK // SUB
    xh[...], xl[...] = halves(all_ref[...])
    wide = 2 * BLOCK
    for i in range(n // wide):
        at, upto = pl.ds(i * wide, wide), pl.ds(0, (i + 1) * wide)
        part = dot3((xh[:, at], xl[:, at]), (xh[:, upto], xl[:, upto]), TN)
        z[at, upto] = part * inv_total
    z[pl.ds(n, nq), :] = q_ref[...]
    z[pl.ds(n + nq, nx), :] = x_ref[...]
    damp = damp_ref[0]
    r = lax.broadcasted_iota(jnp.int32, (BLOCK, BLOCK), 0)
    c = lax.broadcasted_iota(jnp.int32, (BLOCK, BLOCK), 1)
    for b in range(blocks):
        at = pl.ds(b * BLOCK, BLOCK)
        z[at, at] = z[at, at] + jnp.where(r == c, damp, 0.0)
    for ref in (ch, cl, dh, dl, wx):
        ref[...] = jnp.zeros_like(ref)
    out_ref[...] = jnp.zeros_like(out_ref)
    diag[...] = z[pl.ds(0, BLOCK), pl.ds(0, BLOCK)]

    def solve_rows(at, column):
        c_rows = z[at, column]
        w = pair(dot4(pair(c_rows), (dh[...], dl[...]), NT))
        if at.start >= n and at.start < n + nq:
            ch[at, :], cl[at, :] = twice(c_rows)
        if at.start + at.size > n + nq:
            skip = max(n + nq - at.start, 0)
            wx[pl.ds(at.start + skip - n - nq, at.size - skip), :] = w[skip:]
        return w

    def add_scores():
        for j in range(out_ref.shape[0]):
            qs = pl.ds(n + j * cols, cols)
            out_ref[j] += dot4(wx[...], (ch[qs, :], cl[qs, :]), NT)

    def segment(first, last):
        row_lo, col_lo = (first + 1) * BLOCK, first * BLOCK
        step = -(-(rows - row_lo) // (chunks * 16)) * 16
        if (n - row_lo) % step:
            cuts = list(range(row_lo, n, step)) + list(range(n, rows, step)) + [rows]
        else:
            cuts = list(range(row_lo, rows, step)) + [rows]
        spans = [pl.ds(lo, hi - lo) for lo, hi in zip(cuts, cuts[1:])]
        right = pl.ds(col_lo, n - col_lo)

        def body(k, carry):
            column = pl.ds(pl.multiple_of(jnp.maximum(k - 1, 0) * BLOCK, BLOCK), BLOCK)

            def bulk(m):
                mine = spans[m * len(spans) // chunks : (m + 1) * len(spans) // chunks]
                for at in mine:
                    w = solve_rows(at, column)
                    z[at, right] = z[at, right] - dot4(w, (ch[right, :], cl[right, :]), NT)
                if m == chunks - 1:
                    add_scores()

            tiles = [diag[pl.ds(t * SUB, SUB), :] for t in range(chunks)]
            tiles = invert_block(tiles, bulk)
            inverse = jnp.concatenate(tiles, axis=0)
            dh[...], dl[...] = twice(inverse)
            base = pl.multiple_of(k * BLOCK, BLOCK)
            panel = z[right, pl.ds(base, BLOCK)]
            row_at = col_lo + lax.broadcasted_iota(jnp.int32, panel.shape, 0)
            ch[right, :], cl[right, :] = twice(jnp.where(row_at >= base + BLOCK, panel, 0.0))
            nxt = pl.multiple_of(jnp.minimum(k + 1, blocks - 1) * BLOCK, BLOCK)
            at = pl.ds(nxt, BLOCK)
            c_next = z[at, pl.ds(base, BLOCK)]
            w_next = pair(dot4(pair(c_next), twice(inverse), NT))
            diag[...] = z[at, at] - dot4(w_next, twice(c_next), NT)
            return carry

        lax.fori_loop(first, last, body, 0)

    for first in range(0, blocks, 2):
        segment(first, min(first + 2, blocks))
    ends = pl.ds((blocks - 1) * BLOCK, BLOCK)
    solve_rows(pl.ds(n, nq), ends)
    solve_rows(pl.ds(n + nq, nx), ends)
    add_scores()


def eliminate(x_all, damping, x, q, parts):
    total, n = x_all.shape
    rows = n + x.shape[0] + q.shape[0]
    vmem = pl.BlockSpec(memory_space=pltpu.VMEM)
    return pl.pallas_call(
        functools.partial(eliminate_kernel, 1.0 / total),
        out_shape=jax.ShapeDtypeStruct(
            (parts, x.shape[0], q.shape[0] // parts), jnp.float32
        ),
        in_specs=[vmem, pl.BlockSpec(memory_space=pltpu.SMEM), vmem, vmem],
        out_specs=vmem,
        scratch_shapes=[
            pltpu.VMEM((rows, n), jnp.float32),
            pltpu.VMEM((BLOCK, BLOCK), jnp.float32),
            pltpu.VMEM((rows, 2 * BLOCK), jnp.bfloat16),
            pltpu.VMEM((rows, 2 * BLOCK), jnp.bfloat16),
            pltpu.VMEM((BLOCK, 2 * BLOCK), jnp.bfloat16),
            pltpu.VMEM((BLOCK, 2 * BLOCK), jnp.bfloat16),
            pltpu.VMEM((x.shape[0], 2 * BLOCK), jnp.bfloat16),
            pltpu.VMEM((total, n), jnp.bfloat16),
            pltpu.VMEM((total, n), jnp.bfloat16),
        ],
        compiler_params=pltpu.CompilerParams(vmem_limit_bytes=60 * 1024 * 1024),
    )(x_all, damping, x, q)


UP, DOWN, SIDE, CORE = range(4)


def gather_kernel(dims, x_ref, q_ref, x_all, q_all, x_send, x_recv, q_send, q_recv, own_sem):
    line, across, cores = dims
    me = lax.axis_index("ex")
    core = lax.rem(me, cores)
    side = lax.rem(me // cores, across)
    at = me // (cores * across)

    def index(z, y, c):
        return (z * across + y) * cores + c

    has_up, has_down = at < line - 1, at > 0
    targets = {
        UP: index(jnp.minimum(at + 1, line - 1), side, core),
        DOWN: index(jnp.maximum(at - 1, 0), side, core),
        SIDE: index(at, across - 1 - side, core),
        CORE: index(at, side, cores - 1 - core),
    }
    exists = {UP: has_up, DOWN: has_down, SIDE: True, CORE: True}
    kinds = [k for k, on in ((UP, line > 1), (DOWN, line > 1), (SIDE, across > 1), (CORE, cores > 1)) if on]

    def guarded(cond, fn):
        if cond is True:
            fn()
        else:
            pl.when(cond)(fn)

    def both(a, b):
        if a is True:
            return b
        return a if b is True else a & b

    barrier = pltpu.get_barrier_semaphore()
    for kind in kinds:
        def hello(kind=kind):
            pl.semaphore_signal(barrier, inc=1, device_id={"ex": targets[kind]}, device_id_type=MESH)
        guarded(exists[kind], hello)
    peers = sum(1 if exists[k] is True else exists[k].astype(jnp.int32) for k in kinds)
    pl.semaphore_wait(barrier, peers)

    arrays = {"x": (x_ref, x_all, x_send, x_recv), "q": (q_ref, q_all, q_send, q_recv)}
    sent = []

    def copy(name, block, kind, own):
        ref, whole, send, recv = arrays[name]
        height = ref.shape[0]
        rows = whole.at[pl.ds(pl.multiple_of(block * height, 8), height), :]
        return pltpu.make_async_remote_copy(
            src_ref=ref if own else rows, dst_ref=rows,
            send_sem=send.at[block, kind], recv_sem=recv.at[block],
            device_id={"ex": targets[kind]}, device_id_type=MESH,
        )

    def push(name, block, wanted, valid=True, own=False):
        for kind in wanted:
            if kind in kinds:
                cond = both(valid, exists[kind])
                guarded(cond, lambda kind=kind: copy(name, block, kind, own).start())
                sent.append((name, block, kind, own, cond))

    def landed(name, block, valid=True):
        guarded(valid, lambda: copy(name, block, CORE, False).wait_recv())

    def relay(name, block, wanted, valid=True):
        landed(name, block, valid)
        push(name, block, wanted, valid)

    push("x", me, (UP, DOWN, SIDE, CORE), own=True)
    push("q", me, (SIDE, UP, DOWN, CORE), own=True)
    own_copies = []
    for slot, name in enumerate(arrays):
        ref, whole, _, _ = arrays[name]
        height = ref.shape[0]
        own_copies.append(pltpu.make_async_copy(
            ref, whole.at[pl.ds(pl.multiple_of(me * height, 8), height), :], own_sem.at[slot]
        ))
        own_copies[-1].start()
    other = across - 1 - side

    def crossed(s):
        for z, valid in spots(s):
            relay("x", index(z, other, core), (CORE,), valid)

    def spots(s):
        if s == 0:
            return [(at, True)]
        return [
            (jnp.maximum(at - s, 0), at - s >= 0),
            (jnp.minimum(at + s, line - 1), at + s <= line - 1),
        ]

    if across > 1:
        relay("q", index(at, other, core), (UP, DOWN, CORE))
    for s in range(1, line):
        for (z, valid), onward in zip(spots(s), (UP, DOWN)):
            relay("x", index(z, side, core), (onward, SIDE, CORE), valid)
        for (z, valid), onward in zip(spots(s), (UP, DOWN)):
            relay("q", index(z, side, core), (onward, CORE), valid)
            if across > 1:
                relay("q", index(z, other, core), (onward, CORE), valid)
        if across > 1:
            crossed(s - 1)
    if across > 1:
        crossed(line - 1)
    if cores > 1:
        for z in range(line):
            for y in range(across):
                for name in arrays:
                    landed(name, index(z, y, cores - 1 - core))
    for c in own_copies:
        c.wait()
    for name, block, kind, own, cond in sent:
        guarded(cond, lambda: copy(name, block, kind, own).wait_send())


def gather(x, q, dims):
    count = dims[0] * dims[1] * dims[2]
    vmem = pl.BlockSpec(memory_space=pltpu.VMEM)
    hbm = pl.BlockSpec(memory_space=pl.ANY)
    dma = pltpu.SemaphoreType.DMA
    return pl.pallas_call(
        functools.partial(gather_kernel, dims),
        out_shape=[
            jax.ShapeDtypeStruct((count * a.shape[0], a.shape[1]), a.dtype) for a in (x, q)
        ],
        in_specs=[vmem, vmem],
        out_specs=[hbm, hbm],
        scratch_shapes=[dma((count, 4)), dma((count,)), dma((count, 4)), dma((count,)), dma((2,))],
        compiler_params=pltpu.CompilerParams(collective_id=0, has_side_effects=True),
    )(x, q)


def swap_kernel(layers, score_ref, got_ref, send, recv, own_sem):
    me = lax.axis_index("layer")
    barrier = pltpu.get_barrier_semaphore()
    copies = []
    for d in range(1, layers):
        peer = lax.rem(me + d, layers)
        pl.semaphore_signal(barrier, inc=1, device_id={"layer": peer}, device_id_type=MESH)
    own = pltpu.make_async_copy(score_ref.at[me], got_ref.at[me], own_sem)
    own.start()
    pl.semaphore_wait(barrier, layers - 1)
    for d in range(1, layers):
        peer = lax.rem(me + d, layers)
        copies.append(pltpu.make_async_remote_copy(
            src_ref=score_ref.at[peer], dst_ref=got_ref.at[me],
            send_sem=send.at[d], recv_sem=recv.at[d],
            device_id={"layer": peer}, device_id_type=MESH,
        ))
        copies[-1].start()
    for d, c in enumerate(copies, 1):
        c.wait_send()
        source = lax.rem(me + layers - d, layers)
        pltpu.make_async_remote_copy(
            src_ref=score_ref.at[source], dst_ref=got_ref.at[source],
            send_sem=send.at[d], recv_sem=recv.at[d],
            device_id={"layer": source}, device_id_type=MESH,
        ).wait_recv()
    own.wait()


def swap(score):
    layers = score.shape[0]
    if layers == 1:
        return score[0]
    vmem = pl.BlockSpec(memory_space=pltpu.VMEM)
    dma = pltpu.SemaphoreType.DMA
    got = pl.pallas_call(
        functools.partial(swap_kernel, layers),
        out_shape=jax.ShapeDtypeStruct(score.shape, score.dtype),
        in_specs=[vmem],
        out_specs=vmem,
        scratch_shapes=[dma((layers,)), dma((layers,)), dma],
        compiler_params=pltpu.CompilerParams(collective_id=1, has_side_effects=True),
    )(score)
    return jnp.sum(got, axis=0)


def line_dims(mesh):
    axis = mesh.axis_names.index("ex")
    devices = np.moveaxis(mesh.devices, axis, 0).reshape(mesh.shape["ex"], -1)[:, 0]
    count = len(devices)
    places = [tuple(getattr(d, "coords", None) or (i,)) for i, d in enumerate(devices)]
    cores = 2 if count % 2 == 0 and places[0] == places[1] else 1
    chips = places[::cores]
    if len(chips) % 2 or len(chips) < 4:
        return count // cores, 1, cores
    step = [a != b for a, b in zip(chips[0], chips[1])]
    back = [a != b for a, b in zip(chips[0], chips[2])]
    across = 2 if step != back else 1
    return len(chips) // across, across, cores


def solution(mesh):
    dims = line_dims(mesh)

    def on_device(train_grads, query_grads, damping):
        layers_here = train_grads.shape[0]
        parts = lax.axis_size("layer")
        score = None
        for l in range(layers_here):
            x, q = train_grads[l], query_grads[l, 0]
            x_all, q_all = gather(x, q, dims)
            term = eliminate(x_all, damping[l : l + 1], x, q_all, parts)
            score = term if score is None else score + term
        return swap(score)[:, None, :]

    in_specs = (
        P("layer", ("groups", "ex"), None),
        P("layer", "pb", ("groups", "ex"), None),
        P("layer"),
    )
    out_specs = P(("groups", "ex"), "pb", "layer")
    return jax.shard_map(
        on_device, mesh=mesh, in_specs=in_specs, out_specs=out_specs, check_vma=False
    )
```

```python
import functools
import jax
import jax.numpy as jnp
import numpy as np
from jax import lax
from jax.experimental import pallas as pl
from jax.experimental.pallas import tpu as pltpu
from jax.sharding import PartitionSpec as P

BLOCK = 128
SUB = 8
NT = (((1,), (1,)), ((), ()))
NN = (((1,), (0,)), ((), ()))
TN = (((0,), (0,)), ((), ()))
MESH = pl.DeviceIdType.MESH


def halves(x):
    hi = x.astype(jnp.bfloat16)
    return hi, (x - hi.astype(jnp.float32)).astype(jnp.bfloat16)


def dot3(a, b, dims):
    ah, al = a
    bh, bl = b
    dot = functools.partial(
        lax.dot_general, dimension_numbers=dims, preferred_element_type=jnp.float32
    )
    return dot(ah, bh) + (dot(ah, bl) + dot(al, bh))


def pair(x):
    hi, lo = halves(x)
    return jnp.concatenate([hi, lo], axis=1)


def twice(x):
    hi, lo = halves(x)
    return jnp.concatenate([hi, hi], axis=1), jnp.concatenate([lo, lo], axis=1)


def dot4(a, b, dims):
    dot = functools.partial(
        lax.dot_general, dimension_numbers=dims, preferred_element_type=jnp.float32
    )
    return dot(a, b[0]) + dot(a, b[1])


def row_of(x, i):
    return jnp.broadcast_to(x[i : i + 1, :], x.shape)


def lane_of(x, i):
    return jnp.broadcast_to(x[:, i : i + 1], x.shape)


def invert_small(cols):
    sub = lax.broadcasted_iota(jnp.int32, cols[0].shape, 0)
    for j in range(SUB):
        inv = 1.0 / row_of(cols[j], j)
        here = sub == j
        pivot_col = cols[j]
        fresh = []
        for i in range(SUB):
            if i == j:
                fresh.append(jnp.where(here, inv, -pivot_col * inv))
            else:
                scaled = row_of(cols[i], j) * inv
                fresh.append(jnp.where(here, scaled, cols[i] - pivot_col * scaled))
        cols = fresh
    return cols


def invert_block(tiles, between):
    shape = tiles[0].shape
    sub = lax.broadcasted_iota(jnp.int32, shape, 0)
    lane = lax.broadcasted_iota(jnp.int32, shape, 1)
    count = len(tiles)
    for m in range(count):
        c0 = m * SUB
        inside = (lane >= c0) & (lane < c0 + SUB)
        panel = tiles[m]
        cols = invert_small([lane_of(panel, c0 + i) for i in range(SUB)])
        panel = jnp.where(inside, jnp.where(lane == sub + c0, 1.0, 0.0), panel)
        terms = [cols[i] * row_of(panel, i) for i in range(SUB)]
        solved = tree_sum(terms)
        rows = [row_of(solved, i) for i in range(SUB)]
        fresh = list(tiles)
        fresh[m] = solved
        order = [t % count for t in range(m + 1, m + count)]
        for t in order:
            tile = tiles[t]
            terms = [lane_of(tile, c0 + i) * rows[i] for i in range(SUB)]
            fresh[t] = jnp.where(inside, 0.0, tile) - tree_sum(terms)
        tiles = fresh
        between(m)
    return tiles


def tree_sum(terms):
    while len(terms) > 1:
        terms = [a + b for a, b in zip(terms[::2], terms[1::2])]
    return terms[0]


def eliminate_kernel(inv_total, all_ref, damp_ref, x_ref, q_ref, out_ref,
                     z, diag, wp, ch, cl, xh, xl):
    n = all_ref.shape[1]
    nq, nx = q_ref.shape[0], x_ref.shape[0]
    cols = out_ref.shape[2]
    rows = z.shape[0]
    blocks = n // BLOCK
    chunks = BLOCK // SUB
    step = rows // chunks
    xh[...], xl[...] = halves(all_ref[...])
    wide = 2 * BLOCK
    for i in range(n // wide):
        at, upto = pl.ds(i * wide, wide), pl.ds(0, (i + 1) * wide)
        part = dot3((xh[:, at], xl[:, at]), (xh[:, upto], xl[:, upto]), TN)
        z[at, upto] = part * inv_total
    z[pl.ds(n, nq), :] = q_ref[...]
    z[pl.ds(n + nq, nx), :] = x_ref[...]
    if rows > n + nq + nx:
        z[pl.ds(n + nq + nx, rows - n - nq - nx), :] = jnp.zeros(
            (rows - n - nq - nx, n), jnp.float32
        )
    damp = damp_ref[0]
    r = lax.broadcasted_iota(jnp.int32, (BLOCK, BLOCK), 0)
    c = lax.broadcasted_iota(jnp.int32, (BLOCK, BLOCK), 1)
    for b in range(blocks):
        at = pl.ds(b * BLOCK, BLOCK)
        z[at, at] = z[at, at] + jnp.where(r == c, damp, 0.0)
    for ref in (wp, ch, cl):
        ref[...] = jnp.zeros_like(ref)
    out_ref[...] = jnp.zeros_like(out_ref)
    diag[...] = z[pl.ds(0, BLOCK), pl.ds(0, BLOCK)]

    def segment(first, last):
        row_lo, col_lo = (first + 1) * BLOCK, first * BLOCK
        step = (rows - row_lo) // chunks
        right, below = pl.ds(col_lo, n - col_lo), pl.ds(row_lo, rows - row_lo)

        def body(k, carry):
            def bulk(m):
                at = pl.ds(row_lo + m * step, step)
                z[at, right] = z[at, right] - dot4(wp[at, :], (ch[right, :], cl[right, :]), NT)

            tiles = [diag[pl.ds(t * SUB, SUB), :] for t in range(chunks)]
            tiles = invert_block(tiles, bulk)
            inverse = twice(jnp.concatenate(tiles, axis=0))
            base = pl.multiple_of(k * BLOCK, BLOCK)
            panel = z[below, pl.ds(base, BLOCK)]
            row_at = row_lo + lax.broadcasted_iota(jnp.int32, panel.shape, 0)
            panel = jnp.where(row_at >= base + BLOCK, panel, 0.0)
            if first:
                ch[pl.ds(col_lo, BLOCK), :] = jnp.zeros((BLOCK, 2 * BLOCK), jnp.bfloat16)
                cl[pl.ds(col_lo, BLOCK), :] = jnp.zeros((BLOCK, 2 * BLOCK), jnp.bfloat16)
            hi, lo = halves(panel)
            ch[below, :] = jnp.concatenate([hi, hi], axis=1)
            cl[below, :] = jnp.concatenate([lo, lo], axis=1)
            wp[below, :] = pair(dot4(jnp.concatenate([hi, lo], axis=1), inverse, NT))
            nxt = pl.multiple_of(jnp.minimum(k + 1, blocks - 1) * BLOCK, BLOCK)
            at = pl.ds(nxt, BLOCK)
            diag[...] = z[at, at] - dot4(wp[at, :], (ch[at, :], cl[at, :]), NT)
            xs = pl.ds(n + nq, nx)
            for j in range(out_ref.shape[0]):
                qs = pl.ds(n + j * cols, cols)
                out_ref[j] += dot4(wp[xs, :], (ch[qs, :], cl[qs, :]), NT)
            return carry

        lax.fori_loop(first, last, body, 0)

    half = blocks // 2
    segment(0, half)
    segment(half, blocks)


def eliminate(x_all, damping, x, q, parts):
    total, n = x_all.shape
    rows = -(-(n + x.shape[0] + q.shape[0]) // 256) * 256
    vmem = pl.BlockSpec(memory_space=pltpu.VMEM)
    return pl.pallas_call(
        functools.partial(eliminate_kernel, 1.0 / total),
        out_shape=jax.ShapeDtypeStruct(
            (parts, x.shape[0], q.shape[0] // parts), jnp.float32
        ),
        in_specs=[vmem, pl.BlockSpec(memory_space=pltpu.SMEM), vmem, vmem],
        out_specs=vmem,
        scratch_shapes=[
            pltpu.VMEM((rows, n), jnp.float32),
            pltpu.VMEM((BLOCK, BLOCK), jnp.float32),
            pltpu.VMEM((rows, 2 * BLOCK), jnp.bfloat16),
            pltpu.VMEM((rows, 2 * BLOCK), jnp.bfloat16),
            pltpu.VMEM((rows, 2 * BLOCK), jnp.bfloat16),
            pltpu.VMEM((total, n), jnp.bfloat16),
            pltpu.VMEM((total, n), jnp.bfloat16),
        ],
        compiler_params=pltpu.CompilerParams(vmem_limit_bytes=60 * 1024 * 1024),
    )(x_all, damping, x, q)


UP, DOWN, SIDE, CORE = range(4)


def gather_kernel(dims, x_ref, q_ref, x_all, q_all, x_send, x_recv, q_send, q_recv, own_sem):
    line, across, cores = dims
    me = lax.axis_index("ex")
    core = lax.rem(me, cores)
    side = lax.rem(me // cores, across)
    at = me // (cores * across)

    def index(z, y, c):
        return (z * across + y) * cores + c

    has_up, has_down = at < line - 1, at > 0
    targets = {
        UP: index(jnp.minimum(at + 1, line - 1), side, core),
        DOWN: index(jnp.maximum(at - 1, 0), side, core),
        SIDE: index(at, across - 1 - side, core),
        CORE: index(at, side, cores - 1 - core),
    }
    exists = {UP: has_up, DOWN: has_down, SIDE: True, CORE: True}
    kinds = [k for k, on in ((UP, line > 1), (DOWN, line > 1), (SIDE, across > 1), (CORE, cores > 1)) if on]

    def guarded(cond, fn):
        if cond is True:
            fn()
        else:
            pl.when(cond)(fn)

    def both(a, b):
        if a is True:
            return b
        return a if b is True else a & b

    barrier = pltpu.get_barrier_semaphore()
    for kind in kinds:
        def hello(kind=kind):
            pl.semaphore_signal(barrier, inc=1, device_id={"ex": targets[kind]}, device_id_type=MESH)
        guarded(exists[kind], hello)
    peers = sum(1 if exists[k] is True else exists[k].astype(jnp.int32) for k in kinds)
    pl.semaphore_wait(barrier, peers)

    arrays = {"x": (x_ref, x_all, x_send, x_recv), "q": (q_ref, q_all, q_send, q_recv)}
    sent = []

    def copy(name, block, kind, own):
        ref, whole, send, recv = arrays[name]
        height = ref.shape[0]
        rows = whole.at[pl.ds(pl.multiple_of(block * height, 8), height), :]
        return pltpu.make_async_remote_copy(
            src_ref=ref if own else rows, dst_ref=rows,
            send_sem=send.at[block, kind], recv_sem=recv.at[block],
            device_id={"ex": targets[kind]}, device_id_type=MESH,
        )

    def push(name, block, wanted, valid=True, own=False):
        for kind in wanted:
            if kind in kinds:
                cond = both(valid, exists[kind])
                guarded(cond, lambda kind=kind: copy(name, block, kind, own).start())
                sent.append((name, block, kind, own, cond))

    def landed(name, block, valid=True):
        guarded(valid, lambda: copy(name, block, CORE, False).wait_recv())

    def relay(name, block, wanted, valid=True):
        landed(name, block, valid)
        push(name, block, wanted, valid)

    push("x", me, (UP, DOWN, SIDE, CORE), own=True)
    push("q", me, (SIDE, UP, DOWN, CORE), own=True)
    own_copies = []
    for slot, name in enumerate(arrays):
        ref, whole, _, _ = arrays[name]
        height = ref.shape[0]
        own_copies.append(pltpu.make_async_copy(
            ref, whole.at[pl.ds(pl.multiple_of(me * height, 8), height), :], own_sem.at[slot]
        ))
        own_copies[-1].start()
    other = across - 1 - side

    def crossed(s):
        for z, valid in spots(s):
            relay("x", index(z, other, core), (CORE,), valid)

    def spots(s):
        if s == 0:
            return [(at, True)]
        return [
            (jnp.maximum(at - s, 0), at - s >= 0),
            (jnp.minimum(at + s, line - 1), at + s <= line - 1),
        ]

    if across > 1:
        relay("q", index(at, other, core), (UP, DOWN, CORE))
    for s in range(1, line):
        for (z, valid), onward in zip(spots(s), (UP, DOWN)):
            relay("x", index(z, side, core), (onward, SIDE, CORE), valid)
        for (z, valid), onward in zip(spots(s), (UP, DOWN)):
            relay("q", index(z, side, core), (onward, CORE), valid)
            if across > 1:
                relay("q", index(z, other, core), (onward, CORE), valid)
        if across > 1:
            crossed(s - 1)
    if across > 1:
        crossed(line - 1)
    if cores > 1:
        for z in range(line):
            for y in range(across):
                for name in arrays:
                    landed(name, index(z, y, cores - 1 - core))
    for c in own_copies:
        c.wait()
    for name, block, kind, own, cond in sent:
        guarded(cond, lambda: copy(name, block, kind, own).wait_send())


def gather(x, q, dims):
    count = dims[0] * dims[1] * dims[2]
    vmem = pl.BlockSpec(memory_space=pltpu.VMEM)
    hbm = pl.BlockSpec(memory_space=pl.ANY)
    dma = pltpu.SemaphoreType.DMA
    return pl.pallas_call(
        functools.partial(gather_kernel, dims),
        out_shape=[
            jax.ShapeDtypeStruct((count * a.shape[0], a.shape[1]), a.dtype) for a in (x, q)
        ],
        in_specs=[vmem, vmem],
        out_specs=[hbm, hbm],
        scratch_shapes=[dma((count, 4)), dma((count,)), dma((count, 4)), dma((count,)), dma((2,))],
        compiler_params=pltpu.CompilerParams(collective_id=0, has_side_effects=True),
    )(x, q)


def swap_kernel(layers, score_ref, got_ref, send, recv, own_sem):
    me = lax.axis_index("layer")
    barrier = pltpu.get_barrier_semaphore()
    copies = []
    for d in range(1, layers):
        peer = lax.rem(me + d, layers)
        pl.semaphore_signal(barrier, inc=1, device_id={"layer": peer}, device_id_type=MESH)
    own = pltpu.make_async_copy(score_ref.at[me], got_ref.at[me], own_sem)
    own.start()
    pl.semaphore_wait(barrier, layers - 1)
    for d in range(1, layers):
        peer = lax.rem(me + d, layers)
        copies.append(pltpu.make_async_remote_copy(
            src_ref=score_ref.at[peer], dst_ref=got_ref.at[me],
            send_sem=send.at[d], recv_sem=recv.at[d],
            device_id={"layer": peer}, device_id_type=MESH,
        ))
        copies[-1].start()
    for d, c in enumerate(copies, 1):
        c.wait_send()
        source = lax.rem(me + layers - d, layers)
        pltpu.make_async_remote_copy(
            src_ref=score_ref.at[source], dst_ref=got_ref.at[source],
            send_sem=send.at[d], recv_sem=recv.at[d],
            device_id={"layer": source}, device_id_type=MESH,
        ).wait_recv()
    own.wait()


def swap(score):
    layers = score.shape[0]
    if layers == 1:
        return score[0]
    vmem = pl.BlockSpec(memory_space=pltpu.VMEM)
    dma = pltpu.SemaphoreType.DMA
    got = pl.pallas_call(
        functools.partial(swap_kernel, layers),
        out_shape=jax.ShapeDtypeStruct(score.shape, score.dtype),
        in_specs=[vmem],
        out_specs=vmem,
        scratch_shapes=[dma((layers,)), dma((layers,)), dma],
        compiler_params=pltpu.CompilerParams(collective_id=1, has_side_effects=True),
    )(score)
    return jnp.sum(got, axis=0)


def line_dims(mesh):
    axis = mesh.axis_names.index("ex")
    devices = np.moveaxis(mesh.devices, axis, 0).reshape(mesh.shape["ex"], -1)[:, 0]
    count = len(devices)
    places = [tuple(getattr(d, "coords", None) or (i,)) for i, d in enumerate(devices)]
    cores = 2 if count % 2 == 0 and places[0] == places[1] else 1
    chips = places[::cores]
    if len(chips) % 2 or len(chips) < 4:
        return count // cores, 1, cores
    step = [a != b for a, b in zip(chips[0], chips[1])]
    back = [a != b for a, b in zip(chips[0], chips[2])]
    across = 2 if step != back else 1
    return len(chips) // across, across, cores


def solution(mesh):
    dims = line_dims(mesh)

    def on_device(train_grads, query_grads, damping):
        layers_here = train_grads.shape[0]
        parts = lax.axis_size("layer")
        score = None
        for l in range(layers_here):
            x, q = train_grads[l], query_grads[l, 0]
            x_all, q_all = gather(x, q, dims)
            term = eliminate(x_all, damping[l : l + 1], x, q_all, parts)
            score = term if score is None else score + term
        return swap(score)[:, None, :]

    in_specs = (
        P("layer", ("groups", "ex"), None),
        P("layer", "pb", ("groups", "ex"), None),
        P("layer"),
    )
    out_specs = P(("groups", "ex"), "pb", "layer")
    return jax.shard_map(
        on_device, mesh=mesh, in_specs=in_specs, out_specs=out_specs, check_vma=False
    )
```
